32 devices in a mesh: gx: 4 (over y, core), gy: 8 (over z, x).
Axes of the slice: x: 2, y: 2, z: 4, core: 2. Of those that a mesh axis runs over, the one named last changes fastest.
Arguments:
- displacement: float32 [3, 32, 64, 128], P(None, 'gx', 'gy'), may hold values from -0.12 to 0.12
- velocity: float32 [3, 32, 64, 128], P(None, 'gx', 'gy'), may hold values from -4 to 4
- intact: int32 [61, 32, 64, 128], P(None, 'gx', 'gy'), may hold values 0 or 1
- material: int32 [32, 64, 128], P('gx', 'gy'), may hold values from 0 to 7
- bulk_modulus: float32 [8], replicated, may hold values from 80 to 800
- shear_modulus: float32 [8], replicated, may hold values from 40 to 400
- density: float32 [8], replicated, may hold values from 1 to 4
Outputs:
- new_displacement: float32 [3, 32, 64, 128], P(None, 'gx', 'gy')
- new_velocity: float32 [3, 32, 64, 128], P(None, 'gx', 'gy')
- last_force: float32 [3, 32, 64, 128], P(None, 'gx', 'gy')
The draws below stay inside these ranges and needn't reach their ends.
Inputs may be any that keep to these rules, and one draw needn't show every extreme that they name: intact[k, i] refers to the bond from node i to node i + e_k.
All inputs are finite; a program needn't handle non-finite values. No bound on the sum of `intact` on one device may be relied on, other than what follows from the above.
Results may differ from the reference program's by a relative error of at most 0.00002.
Values sent between devices are 32-bit elements; how exact they have to be, the bound alone decides.
A program may use at most 64 MiB of HBM per device.

```python
import math
import jax
import jax.numpy as jnp

NZ = 128
STEPS = 2
BONDS = 61
CLASSES = 8
NX = 32
NY = 64


def set_ends(values, own_key, smallest, largest):
    index_at = [jax.random.randint(jax.random.fold_in(own_key, axis), (), 0, length) for axis, length in enumerate(values.shape)]
    main_axis = values.shape.index(max(values.shape))
    next_to = index_at[:main_axis] + [(index_at[main_axis] + 1) % values.shape[main_axis]] + index_at[main_axis + 1:]
    return values.at[tuple(index_at)].set(smallest).at[tuple(next_to)].set(largest)


def block_scale(stream_key, shape, shards, least, largest):
    level = 1.0
    for dim, blocks in shards:
        steps = jax.random.uniform(jax.random.fold_in(jax.random.fold_in(stream_key, 6), dim), (blocks,), jnp.float32, least / len(shards), largest / len(shards))
        level = level * jnp.repeat(jnp.exp(steps), shape[dim] // blocks).reshape((-1,) + (1,) * (len(shape) - 1 - dim))
    return level


def centred(key, dims, deviation, limit, pieces=(), kind=jnp.bfloat16):
    entries = jax.random.normal(key, dims, jnp.float32) * deviation
    if len(pieces) > 0:
        entries = block_scale(key, dims, pieces, -0.22, 0.18) * entries
    return jnp.clip(entries, min=-limit, max=limit).astype(kind)


def setup_inputs(seed: int = 0) -> dict:
    keys = jax.random.split(jax.random.key(seed), 8)
    displacement = centred(keys[0], (3, NX, NY, NZ), 0.03, 0.12, ((1, 4), (2, 8)), jnp.float32)
    velocity = centred(keys[1], (3, NX, NY, NZ), 1.0, 4.0, ((1, 4), (2, 8)), jnp.float32)
    intact = set_ends((jax.random.randint(keys[2], (BONDS, NX, NY, NZ), 0, 8) < 7).astype(jnp.int32), jax.random.fold_in(keys[2], 1), 0, 1)
    material = set_ends(jax.random.randint(keys[3], (NX, NY, NZ), 0, CLASSES), jax.random.fold_in(keys[3], 1), 0, CLASSES - 1).astype(jnp.int32)
    bulk_modulus = jnp.clip(jnp.exp(jax.random.uniform(keys[4], (CLASSES,), jnp.float32, math.log(80.0), math.log(800.0))), 80.0, 800.0)
    shear_modulus = jnp.clip(jnp.exp(jax.random.uniform(keys[5], (CLASSES,), jnp.float32, math.log(40.0), math.log(400.0))), 40.0, 400.0)
    density = jnp.clip(jnp.exp(jax.random.uniform(keys[6], (CLASSES,), jnp.float32, math.log(1.0), math.log(4.0))), 1.0, 4.0)
    return dict(displacement=displacement, velocity=velocity, intact=intact, material=material, bulk_modulus=bulk_modulus, shear_modulus=shear_modulus, density=density)


time_step = 0.02

def half_offsets():
    result = []
    for along_x in range(-3, 4):
        for along_y in range(-3, 4):
            for along_z in range(-3, 4):
                if along_x * along_x + along_y * along_y + along_z * along_z <= 9 and (along_x, along_y, along_z) > (0, 0, 0):
                    result.append((along_x, along_y, along_z))
    return result

def weighted_volume(offsets):
    return 2.0 * sum((math.sqrt(float(offset[0] * offset[0] + offset[1] * offset[1] + offset[2] * offset[2])) for offset in offsets))

def neighbour(padded, offset, extent):
    return padded[..., 3 + offset[0]:3 + offset[0] + extent[0], 3 + offset[1]:3 + offset[1] + extent[1], 3 + offset[2]:3 + offset[2] + extent[2]]

def stretch_terms(motion, padded_motion, offset, extent):
    partner = neighbour(padded_motion, offset, extent)
    radius = math.sqrt(float(offset[0] * offset[0] + offset[1] * offset[1] + offset[2] * offset[2]))
    components = [offset[number] + partner[number] - motion[number] for number in range(3)]
    length = jnp.sqrt(components[0] * components[0] + components[1] * components[1] + components[2] * components[2])
    return (components, length, length - radius, radius)

def node_force(motion, bulk_node, shear_node, intact, inside, offsets, volume):
    extent = bulk_node.shape
    padded_motion = jnp.pad(motion, ((0, 0), (3, 3), (3, 3), (3, 3)))
    own_sum = jnp.zeros(extent, jnp.float32)
    gathered = jnp.zeros(inside.shape, jnp.float32)
    for bond_index, offset in enumerate(offsets):
        components, length, stretch, radius = stretch_terms(motion, padded_motion, offset, extent)
        weight = intact[bond_index].astype(jnp.float32) * neighbour(inside, offset, extent)
        contribution = weight * stretch
        own_sum = own_sum + contribution
        gathered = gathered.at[3 + offset[0]:3 + offset[0] + extent[0], 3 + offset[1]:3 + offset[1] + extent[1], 3 + offset[2]:3 + offset[2] + extent[2]].add(contribution)
    dilatation = 3.0 / volume * (own_sum + gathered[3:-3, 3:-3, 3:-3])
    pressure = jnp.pad(bulk_node * dilatation, 3)
    shear_padded = jnp.pad(shear_node, 3)
    twisting = jnp.pad(shear_node * dilatation, 3)
    own_force = jnp.zeros(motion.shape, jnp.float32)
    returned = jnp.zeros(padded_motion.shape, jnp.float32)
    for bond_index, offset in enumerate(offsets):
        components, length, stretch, radius = stretch_terms(motion, padded_motion, offset, extent)
        weight = intact[bond_index].astype(jnp.float32) * neighbour(inside, offset, extent)
        tension = weight / radius * (3.0 * radius / volume * (bulk_node * dilatation + neighbour(pressure, offset, extent)) + 15.0 / volume * ((shear_node + neighbour(shear_padded, offset, extent)) * stretch - radius / 3.0 * (shear_node * dilatation + neighbour(twisting, offset, extent))))
        vector = jnp.stack([tension * component / length for component in components])
        own_force = own_force + vector
        returned = returned.at[:, 3 + offset[0]:3 + offset[0] + extent[0], 3 + offset[1]:3 + offset[1] + extent[1], 3 + offset[2]:3 + offset[2] + extent[2]].add(vector)
    return own_force - returned[:, 3:-3, 3:-3, 3:-3]

def reference(displacement, velocity, intact, material, bulk_modulus, shear_modulus, density):
    offsets = half_offsets()
    volume = weighted_volume(offsets)
    bulk_node = bulk_modulus[material]
    shear_node = shear_modulus[material]
    inertia = density[material]
    inside = jnp.pad(jnp.ones(material.shape, jnp.float32), 3)
    forces = jnp.zeros(displacement.shape, jnp.float32)
    for counter in range(STEPS):
        forces = node_force(displacement, bulk_node, shear_node, intact, inside, offsets, volume)
        velocity = velocity + time_step * forces / inertia
        displacement = displacement + time_step * velocity
    return (displacement, velocity, forces)
```

```python
import functools
import math

import jax
import jax.numpy as jnp
from jax import lax
from jax.experimental import pallas as pl
from jax.experimental.pallas import tpu as pltpu
from jax.sharding import PartitionSpec as P

STEPS = 2
TIME_STEP = 0.02
REACH = 3
MESH = pl.DeviceIdType.MESH
F32 = jnp.float32

AROUND = [(dx, dy) for dx in (-1, 0, 1) for dy in (-1, 0, 1) if (dx, dy) != (0, 0)]
SLOT = {direction: number for number, direction in enumerate(AROUND)}
STATE_TO = [(-1, 0), (0, -1), (0, 1), (-1, -1), (-1, 1)]
FINAL_TO = [(1, 0), (0, -1), (0, 1), (1, -1), (1, 1)]


def half_offsets():
    span = range(-REACH, REACH + 1)
    return [
        (a, b, c)
        for a in span
        for b in span
        for c in span
        if a * a + b * b + c * c <= REACH * REACH and (a, b, c) > (0, 0, 0)
    ]


OFFSETS = half_offsets()
GROUPS = {}
for _k, (_a, _b, _c) in enumerate(OFFSETS):
    GROUPS.setdefault((_a, _b), []).append((_k, _c))
RADII = [math.sqrt(float(a * a + b * b + c * c)) for a, b, c in OFFSETS]
VOLUME = 2.0 * sum(RADII)


def round_up(value, unit):
    return -(-value // unit) * unit


def tree_sum(terms):
    while len(terms) > 1:
        terms = [
            terms[n] + terms[n + 1] if n + 1 < len(terms) else terms[n]
            for n in range(0, len(terms), 2)
        ]
    return terms[0]


def kernel(
    grid_rows,
    grid_cols,
    u_ref,
    v_ref,
    intact_hbm,
    mat_ref,
    bulk_ref,
    shear_ref,
    dens_ref,
    out_u,
    out_v,
    out_f,
    intact_ref,
    flag,
    wide_u,
    wide_v,
    u_shift,
    a_shift,
    b_shift,
    a_coef,
    inertia,
    strain,
    force,
    vm,
    pack_u,
    pack_vm,
    pack_t,
    pack_f,
    u_x,
    u_y,
    u_d,
    vm_x,
    vm_y,
    vm_d,
    t_x,
    t_y,
    t_d,
    f_x,
    f_y,
    f_d,
    local_sem,
    send_sem,
    recv_sem,
):
    rows, cols, nz = mat_ref.shape
    wide_rows = rows + REACH
    padded = wide_u.shape[2]
    gx = lax.axis_index("gx")
    gy = lax.axis_index("gy")

    def present(direction):
        x = gx + direction[0]
        y = gy + direction[1]
        return (x >= 0) & (x < grid_rows) & (y >= 0) & (y < grid_cols)

    here = {direction: present(direction) for direction in AROUND}

    load = pltpu.make_async_copy(intact_hbm, intact_ref, local_sem)
    load.start()

    barrier = pltpu.get_barrier_semaphore()
    for direction in AROUND:

        @pl.when(here[direction])
        def _(direction=direction):
            pl.semaphore_signal(
                barrier,
                inc=1,
                device_id=(gx + direction[0], gy + direction[1]),
                device_id_type=MESH,
            )

    for comp in range(3):
        for r in range(rows):
            pack_u[0, comp, 3 * r : 3 * r + 3] = u_ref[comp, r, 0:3]
            pack_u[1, comp, 3 * r : 3 * r + 3] = u_ref[comp, r, cols - 3 : cols]
    vm[0:3] = v_ref[...]
    vm[3] = mat_ref[...].astype(F32)
    for comp in range(4):
        for r in range(rows):
            pack_vm[0, comp, 3 * r : 3 * r + 3] = vm[comp, r, 0:3]
            pack_vm[1, comp, 3 * r : 3 * r + 3] = vm[comp, r, cols - 3 : cols]

    on_x = (gx > 0).astype(jnp.int32) + (gx < grid_rows - 1).astype(jnp.int32)
    on_y = (gy > 0).astype(jnp.int32) + (gy < grid_cols - 1).astype(jnp.int32)
    pl.semaphore_wait(barrier, (1 + on_x) * (1 + on_y) - 1)

    def copy_to(stage, direction, source, target):
        opposite = SLOT[(-direction[0], -direction[1])]
        return pltpu.make_async_remote_copy(
            src_ref=source,
            dst_ref=target,
            send_sem=send_sem.at[stage, SLOT[direction]],
            recv_sem=recv_sem.at[stage, opposite],
            device_id=(gx + direction[0], gy + direction[1]),
            device_id_type=MESH,
        )

    def side(value):
        return 0 if value < 0 else 1

    def state_source(direction, whole, pack):
        dx, dy = direction
        if dy == 0:
            return whole.at[:, 0:REACH]
        if dx == 0:
            return pack.at[side(dy)]
        return pack.at[side(dy), :, 0:16]

    def state_target(origin, x_buf, y_buf, d_buf):
        dx, dy = origin
        if dy == 0:
            return x_buf
        if dx == 0:
            return y_buf.at[side(dy)]
        return d_buf.at[side(dy)]

    def sum_source(direction, whole, pack, final):
        dx, dy = direction
        first = rows if dx > 0 else 0
        lead = (slice(None),)
        if dy == 0:
            return whole.at[lead + (slice(first, first + REACH),)]
        if dx == 0:
            if final:
                return pack.at[(side(dy),) + lead + (slice(0, 6 * rows),)]
            return pack.at[side(dy)]
        return pack.at[(side(dy),) + lead + (slice(6 * first, 6 * first + 24),)]

    def sum_target(origin, x_buf, y_buf, d_buf, step, final):
        dx, dy = origin
        lead = (slice(None),)
        if dy == 0:
            return x_buf.at[step, side(dx)]
        if dx == 0:
            if final:
                return y_buf.at[(step, side(dy)) + lead + (slice(0, 6 * rows),)]
            return y_buf.at[step, side(dy)]
        return d_buf.at[step, 2 * side(dx) + side(dy)]

    def start_all(stage, receivers, source_of, target_of):
        for direction in receivers:

            @pl.when(here[direction])
            def _(direction=direction):
                origin = (-direction[0], -direction[1])
                copy_to(stage, direction, source_of(direction), target_of(origin)).start()

    def wait_recv(stage, direction, source_of, target_of):
        origin = (-direction[0], -direction[1])
        target = target_of(origin)
        pltpu.make_async_remote_copy(
            src_ref=target,
            dst_ref=target,
            send_sem=send_sem.at[stage, SLOT[direction]],
            recv_sem=recv_sem.at[stage, SLOT[origin]],
            device_id=(gx + origin[0], gy + origin[1]),
            device_id_type=MESH,
        ).wait_recv()

    def wait_sends(stage, receivers, source_of, target_of):
        for direction in receivers:

            @pl.when(here[direction])
            def _(direction=direction):
                origin = (-direction[0], -direction[1])
                copy_to(stage, direction, source_of(direction), target_of(origin)).wait_send()

    u_plan = (
        lambda d: state_source(d, u_ref, pack_u),
        lambda o: state_target(o, u_x, u_y, u_d),
    )
    vm_plan = (
        lambda d: state_source(d, vm, pack_vm),
        lambda o: state_target(o, vm_x, vm_y, vm_d),
    )
    start_all(0, STATE_TO, *u_plan)
    start_all(1, STATE_TO, *vm_plan)

    lane = lax.broadcasted_iota(jnp.int32, (padded, nz), 1)

    def shifted(values, c):
        if c == 0:
            return values
        moved = pltpu.roll(values, (-c) % nz, axis=1)
        return jnp.where((lane + c >= 0) & (lane + c < nz), moved, 0.0)

    def take_state(stage, plan, wide_of, comps):
        for direction in STATE_TO:
            origin = (-direction[0], -direction[1])

            @pl.when(here[origin])
            def _(direction=direction, origin=origin):
                wait_recv(stage, direction, *plan)
                dx, dy = origin
                buf = plan[1](origin)
                for comp in range(comps):
                    wide = wide_of(comp)
                    if dy == 0:
                        for r in range(REACH):
                            wide[rows + r, REACH : REACH + cols] = buf[comp, r]
                        continue
                    at = 0 if dy < 0 else REACH + cols
                    for r in range(rows if dx == 0 else REACH):
                        row = r if dx == 0 else rows + r
                        wide[row, at : at + REACH] = buf[comp, 3 * r : 3 * r + 3]

        wait_sends(stage, STATE_TO, *plan)

    wide_u[...] = jnp.zeros(wide_u.shape, F32)
    wide_v[...] = jnp.zeros(wide_v.shape, F32)
    for comp in range(3):
        wide_u[comp, 0:rows, REACH : REACH + cols] = u_ref[comp]
    for comp in range(4):
        wide_v[comp, 0:rows, REACH : REACH + cols] = vm[comp]

    def shift_motion():
        @pl.loop(0, wide_rows)
        def _(r):
            for comp in range(3):
                values = wide_u[comp, r]
                for c in range(-REACH, REACH + 1):
                    moved = shifted(values, c)
                    if comp == 2 and c != 0:
                        moved = moved + float(c)
                    u_shift[c + REACH, comp, r] = moved

    def materials():
        @pl.loop(0, wide_rows)
        def _(r):
            classes = wide_v[3, r]
            bulk = jnp.full(classes.shape, bulk_ref[0], F32)
            shear = jnp.full(classes.shape, shear_ref[0], F32)
            dens = jnp.full(classes.shape, dens_ref[0], F32)
            for number in range(1, bulk_ref.shape[0]):
                match = classes == float(number)
                bulk = jnp.where(match, bulk_ref[number], bulk)
                shear = jnp.where(match, shear_ref[number], shear)
                dens = jnp.where(match, dens_ref[number], dens)
            inertia[r] = TIME_STEP / dens
            a_coef[r] = (9.0 / (VOLUME * VOLUME)) * (bulk - (5.0 / 3.0) * shear)
            stiff = (15.0 / VOLUME) * shear
            for c in range(-REACH, REACH + 1):
                b_shift[c + REACH, r] = shifted(stiff, c)

    depth = lax.broadcasted_iota(jnp.int32, (cols, nz), 1)
    column = lax.broadcasted_iota(jnp.int32, (cols, nz), 0) + gy * cols

    def geometry(i, a, b, c, own):
        at = pl.ds(REACH + b, cols)
        y0 = u_shift[c + REACH, 0, i + a, at] - own[0][a]
        y1 = u_shift[c + REACH, 1, i + a, at] - own[1][b]
        y2 = u_shift[c + REACH, 2, i + a, at] - own[2]
        square = y0 * y0 + y1 * y1 + y2 * y2
        inverse = lax.rsqrt(square)
        return (y0, y1, y2), square * inverse, inverse

    def own_motion(i):
        mine = [wide_u[comp, i, REACH : REACH + cols] for comp in range(3)]
        by_row = {a: mine[0] - float(a) for a in range(REACH + 1)}
        by_col = {b: mine[1] - float(b) for b in range(-REACH, REACH + 1)}
        return (by_row, by_col, mine[2])

    def back(values, c):
        return values if c == 0 else pltpu.roll(values, c % nz, axis=1)

    def strain_pass(first):
        strain[...] = jnp.zeros(strain.shape, F32)

        @pl.loop(0, rows)
        def _(i):
            own = own_motion(i)
            if first:
                lane_in = {
                    c: jnp.where((depth + c >= 0) & (depth + c < nz), 1.0, 0.0)
                    for c in range(-REACH, REACH + 1)
                }
            sums = []
            for (a, b), members in GROUPS.items():
                if first:
                    row_in = (gx * rows + i + a) < grid_rows * rows
                    plane = jnp.where(
                        (column + b >= 0) & (column + b < grid_cols * cols) & row_in, 1.0, 0.0
                    )
                returned = []
                for k, c in members:
                    _, length, _ = geometry(i, a, b, c, own)
                    if first:
                        weight = intact_ref[k, i].astype(F32) * (plane * lane_in[c])
                        flag[k, i] = weight
                    else:
                        weight = flag[k, i]
                    term = weight * (length - RADII[k])
                    sums.append(term)
                    returned.append(back(term, c))
                at = pl.ds(REACH + b, cols)
                strain[0, i + a, at] = strain[0, i + a, at] + tree_sum(returned)
                sums = [tree_sum(sums)]
            at = pl.ds(REACH, cols)
            strain[0, i, at] = strain[0, i, at] + sums[0]

    def force_pass():
        force[...] = jnp.zeros(force.shape, F32)

        @pl.loop(0, rows)
        def _(i):
            own = own_motion(i)
            mid = pl.ds(REACH, cols)
            own_a = a_shift[REACH, i, mid]
            own_b = b_shift[REACH, i, mid]
            sums = [[], [], []]
            for (a, b), members in GROUPS.items():
                at = pl.ds(REACH + b, cols)
                returned = [[], [], []]
                for k, c in members:
                    y, length, inverse = geometry(i, a, b, c, own)
                    both_a = own_a + a_shift[c + REACH, i + a, at]
                    both_b = own_b + b_shift[c + REACH, i + a, at]
                    relative = (length - RADII[k]) * (1.0 / RADII[k])
                    tension = flag[k, i] * (both_a + both_b * relative) * inverse
                    for comp in range(3):
                        term = tension * y[comp]
                        sums[comp].append(term)
                        returned[comp].append(back(term, c))
                for comp in range(3):
                    force[comp, i + a, at] = force[comp, i + a, at] - tree_sum(returned[comp])
                    sums[comp] = [tree_sum(sums[comp])]
            for comp in range(3):
                force[comp, i, mid] = force[comp, i, mid] + sums[comp][0]

    def pack_sums(whole, pack, last_row):
        for comp in range(whole.shape[0]):
            for r in range(last_row):
                pack[0, comp, 6 * r : 6 * r + 6] = whole[comp, r, 0:6]
                pack[1, comp, 6 * r : 6 * r + 6] = whole[comp, r, cols : cols + 6]

    def take_sums(stage, senders, plan, whole, comps, final):
        wait_sends(stage, senders, *plan)
        for direction in senders:
            origin = (-direction[0], -direction[1])

            @pl.when(here[origin])
            def _(direction=direction, origin=origin):
                wait_recv(stage, direction, *plan)
                dx, dy = origin
                buf = plan[1](origin)
                for comp in range(comps):
                    if dy == 0:
                        first = 0 if dx < 0 else rows
                        for r in range(REACH):
                            whole[comp, first + r] = whole[comp, first + r] + buf[comp, r]
                        continue
                    at = pl.ds(0 if dy < 0 else cols, 6)
                    if dx == 0:
                        span = [(r, r) for r in range(rows if final else wide_rows)]
                    else:
                        span = [(r, r + (0 if dx < 0 else rows)) for r in range(REACH)]
                    for r, row in span:
                        whole[comp, row, at] = whole[comp, row, at] + buf[comp, 6 * r : 6 * r + 6]

    take_state(0, u_plan, lambda comp: wide_u.at[comp], 3)
    shift_motion()
    load.wait()

    for step in range(STEPS):
        last = step == STEPS - 1
        strain_pass(step == 0)
        pack_sums(strain, pack_t, wide_rows)
        t_plan = (
            lambda d: sum_source(d, strain, pack_t, False),
            lambda o, step=step: sum_target(o, t_x, t_y, t_d, step, False),
        )
        start_all(2 + 2 * step, AROUND, *t_plan)
        if step == 0:
            take_state(1, vm_plan, lambda comp: wide_v.at[comp], 4)
            materials()
        take_sums(2 + 2 * step, AROUND, t_plan, strain, 1, False)

        @pl.loop(0, wide_rows)
        def _(r):
            values = strain[0, r] * a_coef[r]
            for c in range(-REACH, REACH + 1):
                a_shift[c + REACH, r] = shifted(values, c)

        force_pass()
        pack_sums(force, pack_f, wide_rows)
        receivers = FINAL_TO if last else AROUND
        f_plan = (
            lambda d, last=last: sum_source(d, force, pack_f, last),
            lambda o, step=step, last=last: sum_target(o, f_x, f_y, f_d, step, last),
        )
        start_all(3 + 2 * step, receivers, *f_plan)
        take_sums(3 + 2 * step, receivers, f_plan, force, 3, last)
        if not last:

            @pl.loop(0, wide_rows)
            def _(r):
                for comp in range(3):
                    speed = wide_v[comp, r] + force[comp, r] * inertia[r]
                    wide_v[comp, r] = speed
                    wide_u[comp, r] = wide_u[comp, r] + TIME_STEP * speed

            shift_motion()
        else:
            mid = pl.ds(REACH, cols)

            @pl.loop(0, rows)
            def _(r):
                for comp in range(3):
                    pull = force[comp, r, mid]
                    speed = wide_v[comp, r, mid] + pull * inertia[r, mid]
                    out_f[comp, r] = pull
                    out_v[comp, r] = speed
                    out_u[comp, r] = wide_u[comp, r, mid] + TIME_STEP * speed


def on_device(displacement, velocity, intact, material, bulk_modulus, shear_modulus, density):
    rows, cols, nz = material.shape
    wide_rows = rows + REACH
    padded = round_up(cols + 2 * REACH, 8)
    packed = round_up(6 * wide_rows, 8)
    own = jax.ShapeDtypeStruct((3, rows, cols, nz), F32)
    vmem = pl.BlockSpec(memory_space=pltpu.VMEM)
    smem = pl.BlockSpec(memory_space=pltpu.SMEM)
    stages = 2 + 2 * STEPS

    def buffer(*shape):
        return pltpu.VMEM(shape + (nz,), F32)

    return pl.pallas_call(
        functools.partial(kernel, lax.axis_size("gx"), lax.axis_size("gy")),
        out_shape=(own, own, own),
        in_specs=[vmem, vmem, pl.BlockSpec(memory_space=pl.ANY), vmem, smem, smem, smem],
        out_specs=(vmem, vmem, vmem),
        scratch_shapes=[
            pltpu.VMEM(intact.shape, jnp.int32),
            pltpu.VMEM(intact.shape, F32),
            buffer(3, wide_rows, padded),
            buffer(4, wide_rows, padded),
            buffer(7, 3, wide_rows, padded),
            buffer(7, wide_rows, padded),
            buffer(7, wide_rows, padded),
            buffer(wide_rows, padded),
            buffer(wide_rows, padded),
            buffer(1, wide_rows, padded),
            buffer(3, wide_rows, padded),
            buffer(4, rows, cols),
            buffer(2, 3, 3 * rows),
            buffer(2, 4, 3 * rows),
            buffer(2, 1, packed),
            buffer(2, 3, packed),
            buffer(3, REACH, cols),
            buffer(2, 3, 3 * rows),
            buffer(2, 3, 16),
            buffer(4, REACH, cols),
            buffer(2, 4, 3 * rows),
            buffer(2, 4, 16),
            buffer(STEPS, 2, 1, REACH, padded),
            buffer(STEPS, 2, 1, packed),
            buffer(STEPS, 4, 1, 24),
            buffer(STEPS, 2, 3, REACH, padded),
            buffer(STEPS, 2, 3, packed),
            buffer(STEPS, 4, 3, 24),
            pltpu.SemaphoreType.DMA,
            pltpu.SemaphoreType.DMA((stages, 8)),
            pltpu.SemaphoreType.DMA((stages, 8)),
        ],
        compiler_params=pltpu.CompilerParams(
            collective_id=0, has_side_effects=True, vmem_limit_bytes=48 * 1024 * 1024
        ),
        name="peridynamics",
    )(displacement, velocity, intact, material, bulk_modulus, shear_modulus, density)


def solution(mesh):
    node = P(None, "gx", "gy", None)
    return jax.shard_map(
        on_device,
        mesh=mesh,
        in_specs=(node, node, node, P("gx", "gy", None), P(), P(), P()),
        out_specs=(node, node, node),
        check_vma=False,
    )
```

```python
import functools
import math

import jax
import jax.numpy as jnp
from jax import lax
from jax.experimental import pallas as pl
from jax.experimental.pallas import tpu as pltpu
from jax.sharding import PartitionSpec as P

STEPS = 2
TIME_STEP = 0.02
REACH = 3
NEAR = 2
MESH = pl.DeviceIdType.MESH
F32 = jnp.float32

AROUND = [(dx, dy) for dx in (-1, 0, 1) for dy in (-1, 0, 1) if (dx, dy) != (0, 0)]
STATE = [("S", (-1, 0)), ("S", (0, -1)), ("S", (0, 1)), ("S", (-1, -1)), ("S", (-1, 1))]
CHUNKS = {
    "C": [("C", (1, 0)), ("C", (1, -1)), ("C", (1, 1)), ("C", (0, -1)), ("C", (0, 1))],
    "A": [("A", (-1, 0)), ("A", (-1, -1)), ("A", (-1, 1)), ("A", (0, -1)), ("A", (0, 1))],
    "B": [("B", (0, -1)), ("B", (0, 1))],
}
FINAL = {
    "C": [("C", (1, 0)), ("C", (1, -1)), ("C", (1, 1))],
    "A": [("A", (0, -1)), ("A", (0, 1))],
    "B": [("B", (0, -1)), ("B", (0, 1))],
}
SLOT = {key: n for n, key in enumerate(CHUNKS["C"] + CHUNKS["A"] + CHUNKS["B"])}
SLOT.update({key: n for n, key in enumerate(STATE)})


def half_offsets():
    span = range(-REACH, REACH + 1)
    return [
        (a, b, c)
        for a in span
        for b in span
        for c in span
        if a * a + b * b + c * c <= REACH * REACH and (a, b, c) > (0, 0, 0)
    ]


OFFSETS = half_offsets()
GROUPS = {}
for _k, (_a, _b, _c) in enumerate(OFFSETS):
    GROUPS.setdefault((_a, _b), []).append((_k, _c))
RADII = [math.sqrt(float(a * a + b * b + c * c)) for a, b, c in OFFSETS]
VOLUME = 2.0 * sum(RADII)


def round_up(value, unit):
    return -(-value // unit) * unit


def tree_sum(terms):
    while len(terms) > 1:
        terms = [
            terms[n] + terms[n + 1] if n + 1 < len(terms) else terms[n]
            for n in range(0, len(terms), 2)
        ]
    return terms[0]


def kernel(
    grid_rows,
    grid_cols,
    u_hbm,
    v_hbm,
    intact_hbm,
    mat_hbm,
    bulk_hbm,
    shear_hbm,
    dens_hbm,
    out_u,
    out_v,
    out_f,
    u_ref,
    mat_ref,
    bulk_ref,
    shear_ref,
    dens_ref,
    intact_ref,
    flag,
    by_inverse,
    by_stretch,
    wide_u,
    wide_v,
    u_shift,
    a_shift,
    b_shift,
    a_coef,
    inertia,
    strain,
    force,
    vm,
    pack_u,
    pack_vm,
    pack_t,
    pack_f,
    u_x,
    u_y,
    u_d,
    vm_x,
    vm_y,
    vm_d,
    t_x,
    t_y,
    t_d,
    f_x,
    f_y,
    f_d,
    local_sem,
    send_sem,
    recv_sem,
):
    rows, cols, nz = mat_ref.shape
    wide_rows = rows + REACH
    padded = wide_u.shape[2]
    gx = lax.axis_index("gx")
    gy = lax.axis_index("gy")

    def present(direction):
        x = gx + direction[0]
        y = gy + direction[1]
        return (x >= 0) & (x < grid_rows) & (y >= 0) & (y < grid_cols)

    here = {direction: present(direction) for direction in AROUND}

    barrier = pltpu.get_barrier_semaphore()
    for direction in AROUND:

        @pl.when(here[direction])
        def _(direction=direction):
            pl.semaphore_signal(
                barrier,
                inc=1,
                device_id=(gx + direction[0], gy + direction[1]),
                device_id_type=MESH,
            )

    loads = [
        pltpu.make_async_copy(source, target, local_sem.at[n])
        for n, (source, target) in enumerate(
            [
                (u_hbm, u_ref),
                (v_hbm, vm.at[0:3]),
                (mat_hbm, mat_ref),
                (intact_hbm, intact_ref),
                (bulk_hbm, bulk_ref),
                (shear_hbm, shear_ref),
                (dens_hbm, dens_ref),
            ]
        )
    ]
    for load in loads:
        load.start()

    loads[0].wait()
    for comp in range(3):
        for r in range(rows):
            pack_u[0, comp, 3 * r : 3 * r + 3] = u_ref[comp, r, 0:3]
            pack_u[1, comp, 3 * r : 3 * r + 3] = u_ref[comp, r, cols - 3 : cols]

    on_x = (gx > 0).astype(jnp.int32) + (gx < grid_rows - 1).astype(jnp.int32)
    on_y = (gy > 0).astype(jnp.int32) + (gy < grid_cols - 1).astype(jnp.int32)
    pl.semaphore_wait(barrier, (1 + on_x) * (1 + on_y) - 1)

    def copy_to(stage, key, source, target):
        dx, dy = key[1]
        return pltpu.make_async_remote_copy(
            src_ref=source,
            dst_ref=target,
            send_sem=send_sem.at[stage, SLOT[key]],
            recv_sem=recv_sem.at[stage, SLOT[key]],
            device_id=(gx + dx, gy + dy),
            device_id_type=MESH,
        )

    def side(value):
        return 0 if value < 0 else 1

    def state_source(key, whole, pack):
        dx, dy = key[1]
        if dy == 0:
            return whole.at[:, 0:REACH]
        if dx == 0:
            return pack.at[side(dy)]
        return pack.at[side(dy), :, 0:16]

    def state_target(key, x_buf, y_buf, d_buf):
        dx, dy = key[1]
        if dy == 0:
            return x_buf
        if dx == 0:
            return y_buf.at[side(-dy)]
        return d_buf.at[side(-dy)]

    rows_of = {"A": (0, REACH), "B": (REACH, rows), "C": (rows, wide_rows)}
    wide_a = round_up(6 * REACH, 8)
    wide_b = round_up(6 * (rows - REACH), 8)
    start_of = {"A": 0, "B": wide_a, "C": wide_a + wide_b}

    def packed_rows(chunk, final):
        first, end = rows_of[chunk]
        start = start_of[chunk]
        return slice(start, start + round_up((3 if final else 6) * (end - first), 8))

    def sum_source(key, whole, pack, final):
        chunk, (dx, dy) = key
        if dy == 0:
            return whole.at[:, slice(*rows_of[chunk])]
        return pack.at[side(dy), :, packed_rows(chunk, final)]

    def sum_target(key, x_buf, y_buf, d_buf, step, final):
        chunk, (dx, dy) = key
        if dy == 0:
            return x_buf.at[step, side(-dx)]
        span = packed_rows(chunk, final)
        if dx == 0:
            return y_buf.at[step, side(-dy), :, span]
        return d_buf.at[step, 2 * side(-dx) + side(-dy), :, 0 : span.stop - span.start]

    def start_all(stage, keys, source_of, target_of):
        for key in keys:

            @pl.when(here[key[1]])
            def _(key=key):
                copy_to(stage, key, source_of(key), target_of(key)).start()

    def wait_recv(stage, key, source_of, target_of):
        target = target_of(key)
        pltpu.make_async_remote_copy(
            src_ref=target,
            dst_ref=target,
            send_sem=send_sem.at[stage, SLOT[key]],
            recv_sem=recv_sem.at[stage, SLOT[key]],
            device_id=(gx - key[1][0], gy - key[1][1]),
            device_id_type=MESH,
        ).wait_recv()

    def wait_sends(stage, keys, source_of, target_of):
        for key in keys:

            @pl.when(here[key[1]])
            def _(key=key):
                copy_to(stage, key, source_of(key), target_of(key)).wait_send()

    u_plan = (
        lambda d: state_source(d, u_ref, pack_u),
        lambda o: state_target(o, u_x, u_y, u_d),
    )
    vm_plan = (
        lambda d: state_source(d, vm, pack_vm),
        lambda o: state_target(o, vm_x, vm_y, vm_d),
    )
    start_all(0, STATE, *u_plan)
    loads[1].wait()
    loads[2].wait()
    vm[3] = mat_ref[...].astype(F32)
    for comp in range(4):
        for r in range(rows):
            pack_vm[0, comp, 3 * r : 3 * r + 3] = vm[comp, r, 0:3]
            pack_vm[1, comp, 3 * r : 3 * r + 3] = vm[comp, r, cols - 3 : cols]
    start_all(1, STATE, *vm_plan)

    def shifted(values, c):
        if c == 0:
            return values
        lane = lax.broadcasted_iota(jnp.int32, values.shape, 1)
        moved = pltpu.roll(values, (-c) % nz, axis=1)
        return jnp.where((lane + c >= 0) & (lane + c < nz), moved, 0.0)

    def take_state(stage, plan, wide_of, comps):
        for key in STATE:
            origin = (-key[1][0], -key[1][1])

            @pl.when(here[origin])
            def _(key=key, origin=origin):
                wait_recv(stage, key, *plan)
                dx, dy = origin
                buf = plan[1](key)
                for comp in range(comps):
                    wide = wide_of(comp)
                    if dy == 0:
                        for r in range(REACH):
                            wide[rows + r, REACH : REACH + cols] = buf[comp, r]
                        continue
                    at = 0 if dy < 0 else REACH + cols
                    for r in range(rows if dx == 0 else REACH):
                        row = r if dx == 0 else rows + r
                        wide[row, at : at + REACH] = buf[comp, 3 * r : 3 * r + 3]


    wide_u[...] = jnp.zeros(wide_u.shape, F32)
    wide_v[...] = jnp.zeros(wide_v.shape, F32)
    for comp in range(3):
        wide_u[comp, 0:rows, REACH : REACH + cols] = u_ref[comp]
    for comp in range(4):
        wide_v[comp, 0:rows, REACH : REACH + cols] = vm[comp]

    def shift_motion():
        @pl.loop(0, wide_rows)
        def _(r):
            for comp in range(3):
                values = wide_u[comp, r]
                for c in range(-NEAR, NEAR + 1):
                    moved = shifted(values, c)
                    if comp == 2 and c != 0:
                        moved = moved + float(c)
                    u_shift[c + NEAR, comp, r] = moved

    def materials():
        @pl.loop(0, wide_rows)
        def _(r):
            classes = wide_v[3, r]
            bulk = jnp.full(classes.shape, bulk_ref[0], F32)
            shear = jnp.full(classes.shape, shear_ref[0], F32)
            dens = jnp.full(classes.shape, dens_ref[0], F32)
            for number in range(1, bulk_ref.shape[0]):
                match = classes == float(number)
                bulk = jnp.where(match, bulk_ref[number], bulk)
                shear = jnp.where(match, shear_ref[number], shear)
                dens = jnp.where(match, dens_ref[number], dens)
            inertia[r] = TIME_STEP / dens
            a_coef[r] = (9.0 / (VOLUME * VOLUME)) * (bulk - (5.0 / 3.0) * shear)
            stiff = (15.0 / VOLUME) * shear
            for c in range(-NEAR, NEAR + 1):
                b_shift[c + NEAR, r] = shifted(stiff, c)

    depth = lax.broadcasted_iota(jnp.int32, (cols, nz), 1)
    column = lax.broadcasted_iota(jnp.int32, (cols, nz), 0) + gy * cols

    def partner(buffer, i, a, b, c, own):
        if c > NEAR:
            return shifted(own, c)
        return buffer[c + NEAR, i + a, pl.ds(REACH + b, cols)]

    def bond_vector(i, a, b, c, own):
        y = []
        for comp in range(3):
            if c > NEAR:
                there = shifted(own[3][comp], c)
                if comp == 2:
                    there = there + float(c)
            else:
                there = u_shift[c + NEAR, comp, i + a, pl.ds(REACH + b, cols)]
            y.append(there - (own[0][a], own[1][b], own[2])[comp])
        return y

    def geometry(i, a, b, c, own):
        y0, y1, y2 = bond_vector(i, a, b, c, own)
        square = y0 * y0 + y1 * y1 + y2 * y2
        inverse = lax.rsqrt(square)
        return square * inverse, inverse

    def own_motion(i):
        mine = [wide_u[comp, i, REACH : REACH + cols] for comp in range(3)]
        by_row = {a: mine[0] - float(a) for a in range(REACH + 1)}
        by_col = {b: mine[1] - float(b) for b in range(-REACH, REACH + 1)}
        return (by_row, by_col, mine[2], mine)

    def back(values, c):
        return values if c == 0 else pltpu.roll(values, c % nz, axis=1)

    def order(t):
        return lax.rem(t + rows - REACH, rows)

    def send_done(t, stage, keys, plan, whole, pack, final):
        @pl.when(t == REACH - 1)
        def _():
            pack_sums(whole, pack, "C", final)
            start_all(stage, keys["C"], *plan)

        @pl.when(t == 2 * REACH - 1)
        def _():
            pack_sums(whole, pack, "A", final)
            start_all(stage, keys["A"], *plan)

    def weights():
        @pl.loop(0, rows)
        def _(i):
            lane_in = {
                c: jnp.where((depth + c >= 0) & (depth + c < nz), 1.0, 0.0)
                for c in range(-NEAR, REACH + 1)
            }
            for (a, b), members in GROUPS.items():
                row_in = (gx * rows + i + a) < grid_rows * rows
                plane = jnp.where(
                    (column + b >= 0) & (column + b < grid_cols * cols) & row_in, 1.0, 0.0
                )
                for k, c in members:
                    flag[k, i] = intact_ref[k, i].astype(F32) * (plane * lane_in[c])

    def prepare():
        @pl.loop(0, rows)
        def _(i):
            own_b = b_shift[NEAR, i, pl.ds(REACH, cols)]
            for k, (a, b, c) in enumerate(OFFSETS):
                both_b = own_b + partner(b_shift, i, a, b, c, own_b)
                scale = flag[k, i] * by_inverse[k, i]
                by_stretch[k, i] = scale * (both_b * (by_stretch[k, i] * (1.0 / RADII[k])))
                by_inverse[k, i] = scale

    def strain_pass(send):
        strain[...] = jnp.zeros(strain.shape, F32)

        @pl.loop(0, rows)
        def _(t):
            i = order(t)
            own = own_motion(i)
            sums = []
            for (a, b), members in GROUPS.items():
                returned = []
                for k, c in members:
                    length, inverse = geometry(i, a, b, c, own)
                    stretch = length - RADII[k]
                    by_inverse[k, i] = inverse
                    by_stretch[k, i] = stretch
                    term = flag[k, i] * stretch
                    sums.append(term)
                    returned.append(back(term, c))
                at = pl.ds(REACH + b, cols)
                strain[0, i + a, at] = strain[0, i + a, at] + tree_sum(returned)
                sums = [tree_sum(sums)]
            at = pl.ds(REACH, cols)
            strain[0, i, at] = strain[0, i, at] + sums[0]
            send(t)

    def force_pass(send):
        force[...] = jnp.zeros(force.shape, F32)

        @pl.loop(0, rows)
        def _(t):
            i = order(t)
            own = own_motion(i)
            mid = pl.ds(REACH, cols)
            own_a = a_shift[NEAR, i, mid]
            sums = [[], [], []]
            for (a, b), members in GROUPS.items():
                at = pl.ds(REACH + b, cols)
                returned = [[], [], []]
                for k, c in members:
                    y = bond_vector(i, a, b, c, own)
                    both_a = own_a + partner(a_shift, i, a, b, c, own_a)
                    tension = by_inverse[k, i] * both_a + by_stretch[k, i]
                    for comp in range(3):
                        term = tension * y[comp]
                        sums[comp].append(term)
                        returned[comp].append(back(term, c))
                for comp in range(3):
                    force[comp, i + a, at] = force[comp, i + a, at] - tree_sum(returned[comp])
                    sums[comp] = [tree_sum(sums[comp])]
            for comp in range(3):
                force[comp, i, mid] = force[comp, i, mid] + sums[comp][0]

            send(t)

    def pack_sums(whole, pack, chunk, final):
        first, end = rows_of[chunk]
        start = start_of[chunk]
        width = 3 if final else 6
        high = cols + REACH if final else cols
        for comp in range(whole.shape[0]):
            for n, r in enumerate(range(first, end)):
                at = start + width * n
                pack[0, comp, at : at + width] = whole[comp, r, 0:width]
                pack[1, comp, at : at + width] = whole[comp, r, high : high + width]

    def take_sums(stage, keys, plan, whole, comps, final):
        wait_sends(stage, [key for key in keys["C"] + keys["A"] if key[1][1] == 0], *plan)
        width = 3 if final else 6
        for key in keys["C"] + keys["A"] + keys["B"]:
            chunk, direction = key
            origin = (-direction[0], -direction[1])

            @pl.when(here[origin])
            def _(key=key, chunk=chunk, origin=origin):
                wait_recv(stage, key, *plan)
                dx, dy = origin
                buf = plan[1](key)
                first, end = rows_of[chunk]
                first = first + dx * rows
                for comp in range(comps):
                    for n in range(end - rows_of[chunk][0]):
                        if dy == 0:
                            whole[comp, first + n] = whole[comp, first + n] + buf[comp, n]
                            continue
                        low = REACH if final else 0
                        at = pl.ds(low if dy < 0 else cols, width)
                        whole[comp, first + n, at] = (
                            whole[comp, first + n, at] + buf[comp, width * n : width * n + width]
                        )

    def finish_sends(stage, keys, plan):
        rest = keys["C"] + keys["A"] + keys["B"]
        wait_sends(stage, [key for key in rest if key[1][1] != 0], *plan)

    for load in loads[3:]:
        load.wait()
    weights()
    take_state(0, u_plan, lambda comp: wide_u.at[comp], 3)
    shift_motion()

    for step in range(STEPS):
        last = step == STEPS - 1
        stage = 2 + 2 * step
        t_plan = (
            lambda key: sum_source(key, strain, pack_t, False),
            lambda key, step=step: sum_target(key, t_x, t_y, t_d, step, False),
        )
        strain_pass(
            lambda t, stage=stage, t_plan=t_plan: send_done(
                t, stage, CHUNKS, t_plan, strain, pack_t, False
            ),
        )
        pack_sums(strain, pack_t, "B", False)
        start_all(stage, CHUNKS["B"], *t_plan)
        if step == 0:
            take_state(1, vm_plan, lambda comp: wide_v.at[comp], 4)
            materials()
        prepare()
        take_sums(stage, CHUNKS, t_plan, strain, 1, False)

        @pl.loop(0, wide_rows)
        def _(r):
            values = strain[0, r] * a_coef[r]
            for c in range(-NEAR, NEAR + 1):
                a_shift[c + NEAR, r] = shifted(values, c)

        finish_sends(stage, CHUNKS, t_plan)
        stage = stage + 1
        keys = FINAL if last else CHUNKS
        f_plan = (
            lambda key, last=last: sum_source(key, force, pack_f, last),
            lambda key, step=step, last=last: sum_target(key, f_x, f_y, f_d, step, last),
        )
        force_pass(
            lambda t, stage=stage, keys=keys, f_plan=f_plan, last=last: send_done(
                t, stage, keys, f_plan, force, pack_f, last
            )
        )
        pack_sums(force, pack_f, "B", last)
        start_all(stage, keys["B"], *f_plan)
        take_sums(stage, keys, f_plan, force, 3, last)
        if not last:

            @pl.loop(0, wide_rows)
            def _(r):
                for comp in range(3):
                    speed = wide_v[comp, r] + force[comp, r] * inertia[r]
                    wide_v[comp, r] = speed
                    wide_u[comp, r] = wide_u[comp, r] + TIME_STEP * speed

            shift_motion()
            finish_sends(stage, keys, f_plan)
        else:
            mid = pl.ds(REACH, cols)

            @pl.loop(0, rows)
            def _(r):
                for comp in range(3):
                    pull = force[comp, r, mid]
                    speed = wide_v[comp, r, mid] + pull * inertia[r, mid]
                    out_f[comp, r] = pull
                    out_v[comp, r] = speed
                    out_u[comp, r] = wide_u[comp, r, mid] + TIME_STEP * speed

            finish_sends(stage, keys, f_plan)
            wait_sends(0, STATE, *u_plan)
            wait_sends(1, STATE, *vm_plan)


def hand_over(u_in, v_in, f_in, u_out, v_out, f_out):
    u_out[...] = u_in[...]
    v_out[...] = v_in[...]
    f_out[...] = f_in[...]


def on_device(displacement, velocity, intact, material, bulk_modulus, shear_modulus, density):
    rows, cols, nz = material.shape
    wide_rows = rows + REACH
    padded = round_up(cols + 2 * REACH, 8)
    packed = 2 * round_up(6 * REACH, 8) + round_up(6 * (rows - REACH), 8)
    own = jax.ShapeDtypeStruct((3, rows, cols, nz), F32)
    vmem = pl.BlockSpec(memory_space=pltpu.VMEM)
    hbm = pl.BlockSpec(memory_space=pltpu.HBM)
    table = pltpu.SMEM(bulk_modulus.shape, F32)
    stages = 2 + 2 * STEPS

    def buffer(*shape):
        return pltpu.VMEM(shape + (nz,), F32)

    results = pl.pallas_call(
        functools.partial(kernel, lax.axis_size("gx"), lax.axis_size("gy")),
        out_shape=(own, own, own),
        in_specs=[hbm] * 7,
        out_specs=(vmem, vmem, vmem),
        scratch_shapes=[
            buffer(3, rows, cols),
            pltpu.VMEM(material.shape, jnp.int32),
            table,
            table,
            table,
            pltpu.VMEM(intact.shape, jnp.int32),
            pltpu.VMEM(intact.shape, F32),
            pltpu.VMEM(intact.shape, F32),
            pltpu.VMEM(intact.shape, F32),
            buffer(3, wide_rows, padded),
            buffer(4, wide_rows, padded),
            buffer(5, 3, wide_rows, padded),
            buffer(5, wide_rows, padded),
            buffer(5, wide_rows, padded),
            buffer(wide_rows, padded),
            buffer(wide_rows, padded),
            buffer(1, wide_rows, padded),
            buffer(3, wide_rows, padded),
            buffer(4, rows, cols),
            buffer(2, 3, 3 * rows),
            buffer(2, 4, 3 * rows),
            buffer(2, 1, packed),
            buffer(2, 3, packed),
            buffer(3, REACH, cols),
            buffer(2, 3, 3 * rows),
            buffer(2, 3, 16),
            buffer(4, REACH, cols),
            buffer(2, 4, 3 * rows),
            buffer(2, 4, 16),
            buffer(STEPS, 2, 1, REACH, padded),
            buffer(STEPS, 2, 1, packed),
            buffer(STEPS, 4, 1, 24),
            buffer(STEPS, 2, 3, REACH, padded),
            buffer(STEPS, 2, 3, packed),
            buffer(STEPS, 4, 3, 24),
            pltpu.SemaphoreType.DMA((7,)),
            pltpu.SemaphoreType.DMA((stages, 12)),
            pltpu.SemaphoreType.DMA((stages, 12)),
        ],
        compiler_params=pltpu.CompilerParams(
            collective_id=0, has_side_effects=True, vmem_limit_bytes=67_043_328
        ),
        name="peridynamics",
    )(displacement, velocity, intact, material, bulk_modulus, shear_modulus, density)
    return pl.pallas_call(
        hand_over,
        out_shape=(own, own, own),
        in_specs=[vmem] * 3,
        out_specs=(vmem, vmem, vmem),
        name="hand_over",
    )(*results)


def solution(mesh):
    node = P(None, "gx", "gy", None)
    return jax.shard_map(
        on_device,
        mesh=mesh,
        in_specs=(node, node, node, P("gx", "gy", None), P(), P(), P()),
        out_specs=(node, node, node),
        check_vma=False,
    )
```
